128 devices in a mesh: slab: 4 (over x), tile: 32 (over y, z, core).
Axes of the slice: x: 4, y: 4, z: 4, core: 2. Of those that a mesh axis runs over, the one named last changes fastest.
Arguments:
- features: bfloat16 [262144, 256], P(('slab', 'tile')), may hold values from -24 to 24
- neighbours: int32 [27, 262144], P(None, ('slab', 'tile')), may hold values from 0 to 2303, as said below
- validity: int32 [27, 262144], P(None, ('slab', 'tile')), may hold values from 0 to 1, as said below
- owners: int32 [262144], P(('slab', 'tile')), may hold values from 0 to 127, as said below
- slot_table: int32 [393216], P(('slab', 'tile')), may hold values from 0 to 2048, as said below
- conv_weight: bfloat16 [27, 256, 256], replicated, may hold values from -0.078125 to 0.078125
- cpe_weight: bfloat16 [256, 256], replicated, may hold values from -0.375 to 0.375
- cpe_gain: float32 [256], replicated, may hold values from 0.1 to 1.9
- attn_gain: float32 [256], replicated, may hold values from 0.1 to 1.9
- qkv_weight: bfloat16 [256, 768], replicated, may hold values from -12 to 12
- proj_weight: bfloat16 [256, 256], replicated, may hold values from -0.375 to 0.375
- mlp_gain: float32 [256], replicated, may hold values from 0.1 to 1.9
- mlp_up: bfloat16 [256, 1024], replicated, may hold values from -0.375 to 0.375
- mlp_down: bfloat16 [1024, 256], replicated, may hold values from -0.1875 to 0.1875
Outputs:
- block_out: bfloat16 [262144, 256], P(('slab', 'tile'))
The draws below stay inside these ranges and needn't reach their ends.
Inputs may be any that keep to these rules, and one draw needn't show every extreme that they name: `neighbours`: offset 13 is the row itself (128 + its index in the block). Only the first 128 rows of a block use entries below 128 (offsets 0 to 8), only the last 128 rows use entries above 2048 + 128 - 1 (offsets 18 to 26). `validity`: offset 13 is always 1. `owners`: each device sends at most 24 of its rows to one owner and exactly 24 to some owner; every owner receives 2048 rows in all, exactly 24 of them from some device. `slot_table`: for owner o, entry s * 24 + k is the sequence position of the (k + 1)-th row, in row order, that device s sends to o, and 2048 if s sends o fewer rows; every position 0 to 2047 appears once for each owner.
All inputs are finite; a program needn't handle non-finite values.
Results may differ from the reference program's by a relative error of at most 0.0083.
Values may be sent and summed in bfloat16 or wider, within the bound.
No kernel may reach another device: no remote copies, remote signals or barrier semaphores. Data moves between devices by JAX's collectives and lax.ppermute only.
A program may use at most 128 MiB of HBM per device.

```python
import math
import jax
import jax.numpy as jnp
from jax import lax

C = 256
HEADS = 8
FFN_WIDTH = 1024
PATCH = 1024
KERNEL = 27
ROWS_DEV = 2048
TOTAL = 262144
CAP = 24
RIM = 128
N_SLAB = 4
N_TILE = 32


def routing(key):
    peers = N_SLAB * N_TILE
    row_count = ROWS_DEV
    slot_cap = CAP
    average = row_count // peers
    half_average = average // 2
    keys = jax.random.split(jax.random.fold_in(key, 7), 5)
    shifts = jax.random.randint(keys[0], (peers,), 0, half_average + 1)
    shifts = shifts.at[0].set(half_average).at[1].set(0)
    loads = average + shifts - jnp.roll(shifts, -1)
    sigma = jax.random.permutation(keys[1], peers)
    tau_perm = jax.random.permutation(keys[2], peers)
    counts = loads[(sigma[None, :] - tau_perm[:, None]) % peers]
    cumulative = jnp.cumsum(counts, axis=1)
    entries = jnp.arange(row_count, dtype=jnp.int32)
    dest_sorted = jax.vmap(lambda line: jnp.searchsorted(line, entries, side='right'))(cumulative).astype(jnp.int32)
    row_perms = jax.vmap(lambda sub: jax.random.permutation(sub, row_count))(jax.random.split(keys[3], peers))
    owner_rows = jnp.take_along_axis(dest_sorted, row_perms, axis=1)
    before = jnp.cumsum(counts, axis=0) - counts
    offsets = jnp.arange(slot_cap, dtype=jnp.int32)
    order_index = before.T[:, :, None] + offsets[None, None, :]
    live = offsets[None, None, :] < counts.T[:, :, None]
    owner_perms = jax.vmap(lambda sub: jax.random.permutation(sub, row_count))(jax.random.split(keys[4], peers))
    picked = jnp.take_along_axis(owner_perms, jnp.clip(order_index, 0, row_count - 1).reshape(peers, -1), axis=1)
    table = jnp.where(live.reshape(peers, -1), picked, row_count)
    return (owner_rows.reshape(-1).astype(jnp.int32), table.reshape(-1).astype(jnp.int32))


def draw_owners(key, part):
    return routing(key)[0]


def draw_slot_table(key, part):
    return routing(key)[1]


def draw_neighbours(key, part):
    peers = N_SLAB * N_TILE
    row_count = ROWS_DEV
    rim_rows = RIM
    reach = max(1, min(64, row_count // 4))
    keys = jax.random.split(jax.random.fold_in(key, 11), 3)
    row_ids = jnp.arange(row_count, dtype=jnp.int32)[None, None, :]
    jitter = jax.random.randint(keys[0], (KERNEL, peers, row_count), -reach, reach + 1)
    inside = rim_rows + jnp.clip(row_ids + jitter, 0, row_count - 1)
    below = jax.random.randint(keys[1], (KERNEL, peers, row_count), 0, rim_rows)
    above = row_count + rim_rows + jax.random.randint(keys[2], (KERNEL, peers, row_count), 0, rim_rows)
    offset_ids = jnp.arange(KERNEL, dtype=jnp.int32)[:, None, None]
    chosen = jnp.where((offset_ids < 9) & (row_ids < rim_rows), below, jnp.where((offset_ids >= 18) & (row_ids >= row_count - rim_rows), above, inside))
    chosen = jnp.where(offset_ids == 13, rim_rows + row_ids, chosen)
    return chosen.reshape(KERNEL, peers * row_count).astype(jnp.int32)


def draw_validity(key, part):
    rolled = jax.random.randint(jax.random.fold_in(key, 13), (KERNEL, TOTAL), 0, 4)
    flags = (rolled < 3).astype(jnp.int32)
    return flags.at[13].set(1)


def draw_features(key, part):
    keys = jax.random.split(jax.random.fold_in(key, 17), 3)
    column_scale = jnp.exp(jax.random.uniform(keys[1], (1, C), jnp.float32, math.log(0.3), math.log(3.0)))
    row_scale = jnp.exp(jax.random.uniform(keys[2], (TOTAL, 1), jnp.float32, math.log(0.5), math.log(2.0)))
    base = jax.random.normal(keys[0], (TOTAL, C), jnp.float32)
    return (jnp.clip(base, -4.0, 4.0) * row_scale * column_scale).astype(jnp.bfloat16)


def draw_qkv_weight(key, part):
    keys = jax.random.split(jax.random.fold_in(key, 19), 1)
    base = jnp.clip(jax.random.normal(keys[0], (C, 3 * C), jnp.float32), -4.0, 4.0) / math.sqrt(C)
    return jnp.clip(base, -12.0, 12.0).astype(jnp.bfloat16)


def scatter_about(key, dims, scale, most, kind=jnp.bfloat16):
    return jnp.clip(scale * jax.random.normal(key, dims, jnp.float32), -most, most).astype(kind)


def setup_inputs(seed: int = 0) -> dict:
    key_of = jax.random.split(jax.random.key(seed), 15)
    features = draw_features(jax.random.fold_in(key_of[14], 71), 0)
    neighbours = draw_neighbours(jax.random.fold_in(key_of[14], 71), 0)
    validity = draw_validity(jax.random.fold_in(key_of[14], 71), 0)
    owners = draw_owners(jax.random.fold_in(key_of[14], 71), 0)
    slot_table = draw_slot_table(jax.random.fold_in(key_of[14], 71), 0)
    conv_weight = scatter_about(key_of[5], (KERNEL, C, C), (KERNEL * C) ** -0.5, 0.078125)
    cpe_weight = scatter_about(key_of[6], (C, C), C ** -0.5, 0.375)
    cpe_gain = jnp.clip(1.0 + 0.18 * jax.random.normal(key_of[7], (C,), jnp.float32), 0.1, 1.9)
    attn_gain = jnp.clip(1.0 + 0.18 * jax.random.normal(key_of[8], (C,), jnp.float32), 0.1, 1.9)
    qkv_weight = draw_qkv_weight(jax.random.fold_in(key_of[14], 71), 0)
    proj_weight = scatter_about(key_of[10], (C, C), C ** -0.5, 0.375)
    mlp_gain = jnp.clip(1.0 + 0.18 * jax.random.normal(key_of[11], (C,), jnp.float32), 0.1, 1.9)
    mlp_up = scatter_about(key_of[12], (C, FFN_WIDTH), C ** -0.5, 0.375)
    mlp_down = scatter_about(key_of[13], (FFN_WIDTH, C), FFN_WIDTH ** -0.5, 0.1875)
    return {"features": features, "neighbours": neighbours, "validity": validity, "owners": owners, "slot_table": slot_table, "conv_weight": conv_weight, "cpe_weight": cpe_weight, "cpe_gain": cpe_gain, "attn_gain": attn_gain, "qkv_weight": qkv_weight, "proj_weight": proj_weight, "mlp_gain": mlp_gain, "mlp_up": mlp_up, "mlp_down": mlp_down}


EPS = 1e-05

def layer_norm(values, gain):
    centred = values - lax.optimization_barrier(jnp.mean(values, axis=-1, keepdims=True))
    spread = lax.optimization_barrier(jnp.mean(centred * centred, axis=-1, keepdims=True))
    return centred * lax.rsqrt(spread + EPS) * gain.astype(values.dtype)

def conv_block(extended, index_rows, keep_rows, conv_weight):

    def add_offset(running, parts):
        index, keep, weight = parts
        picked = jnp.where(keep[:, None] > 0, extended[index], jnp.zeros((), extended.dtype))
        return (running + jnp.dot(picked, weight, preferred_element_type=jnp.float32), None)
    begin = jnp.zeros((index_rows.shape[1], extended.shape[1]), jnp.float32)
    result, _ = lax.scan(add_offset, begin, (index_rows, keep_rows, conv_weight))
    return result

def embed(row_feats, conv_sum, cpe_weight, cpe_gain):
    linear = jnp.dot(conv_sum.astype(jnp.bfloat16), cpe_weight, preferred_element_type=jnp.float32)
    return (row_feats.astype(jnp.float32) + layer_norm(linear, cpe_gain)).astype(jnp.bfloat16)

def send_positions(dest, peers, slot_cap):
    hits = (dest[:, None] == jnp.arange(peers, dtype=jnp.int32)[None, :]).astype(jnp.int32)
    peer_rank = lax.optimization_barrier(jnp.sum((jnp.cumsum(hits, axis=0) - 1) * hits, axis=1)).astype(jnp.int32)
    return (dest * slot_cap + peer_rank).astype(jnp.int32)

def attend_block(sequence, attn_gain, qkv_weight, proj_weight, mlp_gain, mlp_up, mlp_down):
    row_count = sequence.shape[0]
    feat_width = sequence.shape[1]
    head_dim = feat_width // HEADS
    normed = layer_norm(sequence.astype(jnp.float32), attn_gain).astype(jnp.bfloat16)
    packed = jnp.dot(normed, qkv_weight, preferred_element_type=jnp.float32).astype(jnp.bfloat16)
    block_rows = min(512, PATCH)
    starts = jnp.arange(row_count // block_rows, dtype=jnp.int32) * block_rows
    score_scale = 1.0 / math.sqrt(head_dim)

    def one_block(block_start):
        patch_first = block_start // PATCH * PATCH
        queries = lax.dynamic_slice_in_dim(packed, block_start, block_rows, 0)[:, :feat_width]
        queries = queries.reshape(block_rows, HEADS, head_dim).astype(jnp.float32)
        patch_rows = lax.dynamic_slice_in_dim(packed, patch_first, PATCH, 0)
        key_rows = patch_rows[:, feat_width:2 * feat_width].reshape(PATCH, HEADS, head_dim).astype(jnp.float32)
        value_rows = patch_rows[:, 2 * feat_width:].reshape(PATCH, HEADS, head_dim).astype(jnp.float32)
        scores = jnp.einsum('qhd,khd->hqk', queries, key_rows) * score_scale
        row_peak = lax.optimization_barrier(jnp.max(scores, axis=-1, keepdims=True))
        raised = jnp.exp(scores - row_peak)
        weights = (raised / lax.optimization_barrier(jnp.sum(raised, axis=-1, keepdims=True))).astype(jnp.bfloat16)
        mixed_heads = jnp.einsum('hqk,khd->qhd', weights.astype(jnp.float32), value_rows)
        return mixed_heads.astype(jnp.bfloat16).reshape(block_rows, feat_width)
    attended = lax.map(one_block, starts).reshape(row_count, feat_width)
    after_attn = (sequence.astype(jnp.float32) + jnp.dot(attended, proj_weight, preferred_element_type=jnp.float32)).astype(jnp.bfloat16)
    normed_two = layer_norm(after_attn.astype(jnp.float32), mlp_gain).astype(jnp.bfloat16)
    hidden_act = jax.nn.gelu(jnp.dot(normed_two, mlp_up, preferred_element_type=jnp.float32), approximate=True).astype(jnp.bfloat16)
    return (after_attn.astype(jnp.float32) + jnp.dot(hidden_act, mlp_down, preferred_element_type=jnp.float32)).astype(jnp.bfloat16)

def reference(features, neighbours, validity, owners, slot_table, conv_weight, cpe_weight, cpe_gain, attn_gain, qkv_weight, proj_weight, mlp_gain, mlp_up, mlp_down):
    devices = N_SLAB * N_TILE
    feat_width = features.shape[1]
    grid = features.reshape(N_SLAB, N_TILE, ROWS_DEV, feat_width)
    blank = jnp.zeros((1, N_TILE, RIM, feat_width), features.dtype)
    lower = jnp.concatenate([blank, grid[:-1, :, ROWS_DEV - RIM:]], axis=0)
    upper = jnp.concatenate([grid[1:, :, :RIM], blank], axis=0)
    extended = jnp.concatenate([lower, grid, upper], axis=2).reshape(devices, ROWS_DEV + 2 * RIM, feat_width)
    index_all = neighbours.reshape(KERNEL, devices, ROWS_DEV).transpose(1, 0, 2)
    keep_all = validity.reshape(KERNEL, devices, ROWS_DEV).transpose(1, 0, 2)
    own_rows = features.reshape(devices, ROWS_DEV, feat_width)

    def embed_device(parts):
        ext_rows, index_rows, keep_rows, row_feats = parts
        return embed(row_feats, conv_block(ext_rows, index_rows, keep_rows, conv_weight), cpe_weight, cpe_gain)
    embedded = lax.map(embed_device, (extended, index_all, keep_all, own_rows))
    slot_cap = slot_table.shape[0] // (devices * devices)
    owner_rows = owners.reshape(devices, ROWS_DEV)
    send_slots = lax.map(lambda dest: send_positions(dest, devices, slot_cap), owner_rows)
    outgoing = jax.vmap(lambda slots, rows: jnp.zeros((devices * slot_cap, feat_width), jnp.bfloat16).at[slots].set(rows))(send_slots, embedded)
    arrived = outgoing.reshape(devices, devices, slot_cap, feat_width).transpose(1, 0, 2, 3).reshape(devices, devices * slot_cap, feat_width)
    table = slot_table.reshape(devices, devices * slot_cap)
    sequence = jax.vmap(lambda places, rows: jnp.zeros((ROWS_DEV, feat_width), jnp.bfloat16).at[places].set(rows, mode='drop'))(table, arrived)
    processed = attend_block(sequence.reshape(devices * ROWS_DEV, feat_width), attn_gain, qkv_weight, proj_weight, mlp_gain, mlp_up, mlp_down)
    processed = processed.reshape(devices, ROWS_DEV, feat_width)
    leaving = jax.vmap(lambda rows, places: rows[jnp.minimum(places, ROWS_DEV - 1)])(processed, table)
    returned = leaving.reshape(devices, devices, slot_cap, feat_width).transpose(1, 0, 2, 3).reshape(devices, devices * slot_cap, feat_width)
    result = jax.vmap(lambda rows, slots: rows[slots])(returned, send_slots)
    return result.reshape(devices * ROWS_DEV, feat_width)
```

```python
import math

import jax
import jax.numpy as jnp
from jax import lax
from jax.experimental import pallas as pl
from jax.experimental.pallas import tpu as pltpu
from jax.sharding import PartitionSpec as P

EPS = 1e-05
F32 = jnp.float32
BF16 = jnp.bfloat16
I32 = jnp.int32

C = 256
HEADS = 8
HEAD_DIM = 32
PATCH = 1024
ROWS = 2048
RIM = 128
PEERS = 128
CAP = 24
SLOTS = PEERS * CAP
OFFSETS = 27
GROUP = 9
BLOCK = 128
WINDOW = 256
SUPER = 512
QBLOCK = 512
SCORE_SCALE = math.log2(math.e) / math.sqrt(HEAD_DIM)
VMEM_LIMIT = 60 << 20


def dot(a, b):
    return jnp.dot(a, b, preferred_element_type=F32)


def dot_nt(a, b):
    return lax.dot_general(a, b, (((1,), (1,)), ((), ())), preferred_element_type=F32)


def layer_norm(values, gain):
    centred = values - jnp.mean(values, axis=-1, keepdims=True)
    spread = jnp.mean(centred * centred, axis=-1, keepdims=True)
    return centred * lax.rsqrt(spread + EPS) * gain


def whole(shape):
    return pl.BlockSpec(shape, lambda i, *_: (0,) * len(shape))


def conv_kernel(
    first_ref, count_ref, own, lower, upper, index, owners, weight, cpe, gain,
    outgoing, slot, ext, select, picked, emb,
):
    step = pl.program_id(0)
    blocks = SUPER // BLOCK

    @pl.when(step == 0)
    def _():
        ext[0:RIM, :] = lower[...]
        ext[RIM : RIM + ROWS, :] = own[...]
        ext[RIM + ROWS : 2 * RIM + ROWS, :] = upper[...]
        ext[2 * RIM + ROWS :, :] = jnp.zeros((WINDOW, C), BF16)

    lanes = lax.broadcasted_iota(I32, (BLOCK, WINDOW), 1).astype(F32)

    def one_block(b, carry):
        row = pl.multiple_of(step * SUPER + b * BLOCK, BLOCK)
        place = pl.multiple_of(b * BLOCK, BLOCK)
        columns = jnp.transpose(index[:, pl.ds(row, BLOCK)].astype(F32), (1, 0))
        for g in range(OFFSETS // GROUP):
            entry = g * (ROWS // BLOCK) + step * blocks + b
            first = first_ref[entry]

            def window(t):
                base = pl.multiple_of(first + t * WINDOW, 16)
                shift = base.astype(F32)
                for k in range(GROUP):
                    rel = columns[:, GROUP * g + k : GROUP * g + k + 1] - shift
                    select[k * BLOCK : (k + 1) * BLOCK, :] = jnp.where(rel == lanes, 1.0, 0.0).astype(BF16)
                rows = dot(select[...], ext[pl.ds(base, WINDOW), :]).astype(BF16)
                out = []
                for k in range(GROUP):
                    col = (GROUP * g + k) * C
                    out.append(((pl.ds(place, BLOCK), slice(col, col + C)), rows[k * BLOCK : (k + 1) * BLOCK, :]))
                return out

            for dst, rows in window(0):
                picked[dst] = rows

            def more(t, carry):
                for dst, rows in window(t):
                    picked[dst] = picked[dst] + rows
                return carry

            lax.fori_loop(1, count_ref[entry], more, 0)
        return carry

    lax.fori_loop(0, blocks, one_block, 0)
    at = pl.multiple_of(step * SUPER, SUPER)
    linear = dot(dot(picked[...], weight[...]).astype(BF16), cpe[...])
    emb[pl.ds(at, SUPER), :] = (
        own[pl.ds(at, SUPER), :].astype(F32) + layer_norm(linear, gain[...])
    ).astype(BF16)

    @pl.when(step == ROWS // SUPER - 1)
    def _():
        width = 256
        peer = lax.broadcasted_iota(I32, (PEERS, width), 0)
        before = lax.broadcasted_iota(I32, (width, width), 0) < lax.broadcasted_iota(I32, (width, width), 1)
        before = jnp.where(before, 1.0, 0.0).astype(BF16)
        base = jnp.zeros((PEERS, 1), F32)
        for c in range(ROWS // width):
            cols = slice(c * width, (c + 1) * width)
            owner = owners[:, cols]
            hits = jnp.where(peer == owner, 1.0, 0.0)
            seen = dot(hits.astype(BF16), before) + base
            rank = jnp.sum(hits * seen, axis=0, keepdims=True)
            slot[:, cols] = owner * CAP + rank.astype(I32)
            base = base + jnp.sum(hits, axis=1, keepdims=True)
        chunk = 256
        places = lax.broadcasted_iota(I32, (chunk, ROWS), 0)
        for c in range(SLOTS // chunk):
            pick = jnp.where(slot[...] - c * chunk == places, 1.0, 0.0).astype(BF16)
            outgoing[c * chunk : (c + 1) * chunk, :] = dot(pick, emb[...]).astype(BF16)


def conv_part(features, lower, upper, neighbours, validity, owners, conv_weight, cpe_weight, cpe_gain):
    index = jnp.where(validity > 0, neighbours, -1)
    split = (OFFSETS // GROUP, GROUP, ROWS // BLOCK, BLOCK)
    low = jnp.min(jnp.where(validity > 0, neighbours, 2 * ROWS).reshape(split), axis=(1, 3))
    high = jnp.max(index.reshape(split), axis=(1, 3))
    low = jnp.minimum(low, ROWS + 2 * RIM - 1) // 16 * 16
    count = (high - low + WINDOW) // WINDOW
    index = jnp.pad(index, ((0, 5), (0, 0)), constant_values=-1)
    args = (
        features, lower, upper, index, owners.reshape(1, ROWS), conv_weight.reshape(OFFSETS * C, C),
        cpe_weight, cpe_gain.reshape(1, C),
    )
    return pl.pallas_call(
        conv_kernel,
        grid_spec=pltpu.PrefetchScalarGridSpec(
            num_scalar_prefetch=2,
            grid=(ROWS // SUPER,),
            in_specs=[whole(a.shape) for a in args],
            out_specs=[whole((SLOTS, C)), whole((1, ROWS))],
            scratch_shapes=[
                pltpu.VMEM((ROWS + 2 * RIM + WINDOW, C), BF16),
                pltpu.VMEM((GROUP * BLOCK, WINDOW), BF16),
                pltpu.VMEM((SUPER, OFFSETS * C), BF16),
                pltpu.VMEM((ROWS, C), BF16),
            ],
        ),
        out_shape=[jax.ShapeDtypeStruct((SLOTS, C), BF16), jax.ShapeDtypeStruct((1, ROWS), I32)],
        compiler_params=pltpu.CompilerParams(vmem_limit_bytes=VMEM_LIMIT),
        name="conv_part",
    )(low.reshape(-1), count.reshape(-1), *args)


def attend_kernel(
    arrived, table_row, table_col, attn_gain, qkv, proj, mlp_gain, up, down,
    leaving, seq, processed, keys, queries, values, mixed, scores_a, scores_b, peak_a, peak_b,
):
    patch = pl.program_id(0)
    chunk = 256
    places = lax.broadcasted_iota(I32, (chunk, SLOTS), 0)
    for c in range(PATCH // chunk):
        pick = jnp.where(table_row[...] - (patch * PATCH + c * chunk) == places, 1.0, 0.0).astype(BF16)
        seq[c * chunk : (c + 1) * chunk, :] = dot(pick, arrived[...])
    normed = layer_norm(seq[...], attn_gain[...]).astype(BF16)
    queries[...] = dot_nt(jnp.transpose(qkv[:, 0:C], (1, 0)), normed).astype(BF16)
    key_rows = dot(normed, qkv[:, C : 2 * C]).astype(BF16)
    value_cols = dot_nt(jnp.transpose(qkv[:, 2 * C :], (1, 0)), normed).astype(BF16)
    for h in range(HEADS):
        keys[h, :, :] = key_rows[:, HEAD_DIM * h : HEAD_DIM * (h + 1)]
        values[h, 0:HEAD_DIM, :] = value_cols[HEAD_DIM * h : HEAD_DIM * (h + 1), :]
        values[h, HEAD_DIM:, :] = jnp.ones((16, PATCH), BF16)
    per_head = PATCH // QBLOCK
    tasks = HEADS * per_head

    def where_is(t):
        head = lax.div(t, per_head)
        return (
            head,
            pl.multiple_of(head * HEAD_DIM, HEAD_DIM),
            pl.multiple_of(lax.rem(t, per_head) * QBLOCK, QBLOCK),
        )

    def score(t, scores, peak):
        head, row, col = where_is(lax.rem(t, tasks))
        found = dot(keys[head], queries[pl.ds(row, HEAD_DIM), pl.ds(col, QBLOCK)])
        scores[...] = found
        peak[...] = jnp.max(found, axis=0, keepdims=True)

    def mix(t, scores, peak):
        head, row, col = where_is(t)
        raised = jnp.exp2((scores[...] - peak[...]) * SCORE_SCALE).astype(BF16)
        total = dot(values[head], raised)
        mixed[pl.ds(row, HEAD_DIM), pl.ds(col, QBLOCK)] = total[0:HEAD_DIM, :] / total[HEAD_DIM : HEAD_DIM + 1, :]

    score(0, scores_a, peak_a)

    def two(u, carry):
        t = 2 * u
        score(t + 1, scores_b, peak_b)
        mix(t, scores_a, peak_a)
        score(t + 2, scores_a, peak_a)
        mix(t + 1, scores_b, peak_b)
        return carry

    lax.fori_loop(0, tasks // 2, two, 0)
    attended = jnp.transpose(mixed[...], (1, 0)).astype(BF16)
    after = (seq[...] + dot(attended, proj[...])).astype(BF16).astype(F32)
    normed_two = layer_norm(after, mlp_gain[...]).astype(BF16)
    hidden = jax.nn.gelu(dot(normed_two, up[...]), approximate=True).astype(BF16)
    at = pl.multiple_of(patch * PATCH, PATCH)
    processed[pl.ds(at, PATCH), :] = (after + dot(hidden, down[...])).astype(BF16)

    @pl.when(patch == ROWS // PATCH - 1)
    def _():
        lanes = lax.broadcasted_iota(I32, (chunk, ROWS), 1)
        for c in range(SLOTS // chunk):
            rows = slice(c * chunk, (c + 1) * chunk)
            pick = jnp.where(table_col[rows, :] == lanes, 1.0, 0.0).astype(BF16)
            leaving[rows, :] = dot(pick, processed[...]).astype(BF16)


def attend_part(arrived, slot_table, attn_gain, qkv_weight, proj_weight, mlp_gain, mlp_up, mlp_down):
    args = (
        arrived, slot_table.reshape(1, SLOTS), slot_table.reshape(SLOTS, 1), attn_gain.reshape(1, C),
        qkv_weight, proj_weight, mlp_gain.reshape(1, C), mlp_up, mlp_down,
    )
    return pl.pallas_call(
        attend_kernel,
        grid=(ROWS // PATCH,),
        in_specs=[whole(a.shape) for a in args],
        out_specs=whole((SLOTS, C)),
        out_shape=jax.ShapeDtypeStruct((SLOTS, C), BF16),
        scratch_shapes=[
            pltpu.VMEM((PATCH, C), F32),
            pltpu.VMEM((ROWS, C), BF16),
            pltpu.VMEM((HEADS, PATCH, HEAD_DIM), BF16),
            pltpu.VMEM((C, PATCH), BF16),
            pltpu.VMEM((HEADS, HEAD_DIM + 16, PATCH), BF16),
            pltpu.VMEM((C, PATCH), F32),
            pltpu.VMEM((PATCH, QBLOCK), F32),
            pltpu.VMEM((PATCH, QBLOCK), F32),
            pltpu.VMEM((1, QBLOCK), F32),
            pltpu.VMEM((1, QBLOCK), F32),
        ],
        compiler_params=pltpu.CompilerParams(vmem_limit_bytes=VMEM_LIMIT),
        name="attend_part",
    )(*args)


def return_kernel(returned, slot_col, out):
    lanes = lax.broadcasted_iota(I32, (out.shape[0], SLOTS), 1)
    pick = jnp.where(slot_col[...] == lanes, 1.0, 0.0).astype(BF16)
    out[...] = dot(pick, returned[...]).astype(BF16)


def return_part(returned, slot):
    rows = 512
    return pl.pallas_call(
        return_kernel,
        grid=(ROWS // rows,),
        in_specs=[whole((SLOTS, C)), pl.BlockSpec((rows, 1), lambda i: (i, 0))],
        out_specs=pl.BlockSpec((rows, C), lambda i: (i, 0)),
        out_shape=jax.ShapeDtypeStruct((ROWS, C), BF16),
        compiler_params=pltpu.CompilerParams(vmem_limit_bytes=VMEM_LIMIT),
        name="return_part",
    )(returned, slot.reshape(ROWS, 1))


def exchange(rows):
    return lax.all_to_all(
        rows.reshape(PEERS, CAP, C), ("slab", "tile"), split_axis=0, concat_axis=0, tiled=True
    ).reshape(SLOTS, C)


def local(
    features, neighbours, validity, owners, slot_table, conv_weight, cpe_weight, cpe_gain,
    attn_gain, qkv_weight, proj_weight, mlp_gain, mlp_up, mlp_down,
):
    slabs = lax.axis_size("slab")
    lower = lax.ppermute(features[ROWS - RIM :], "slab", [(i, i + 1) for i in range(slabs - 1)])
    upper = lax.ppermute(features[:RIM], "slab", [(i + 1, i) for i in range(slabs - 1)])
    outgoing, slot = conv_part(
        features, lower, upper, neighbours, validity, owners, conv_weight, cpe_weight, cpe_gain
    )
    leaving = attend_part(
        exchange(outgoing), slot_table, attn_gain, qkv_weight, proj_weight, mlp_gain, mlp_up, mlp_down
    )
    return return_part(exchange(leaving), slot)


def solution(mesh):
    both = P(("slab", "tile"))
    in_specs = (
        P(("slab", "tile"), None), P(None, ("slab", "tile")), P(None, ("slab", "tile")), both, both,
    ) + (P(),) * 9
    mapped = jax.shard_map(
        local, mesh=mesh, in_specs=in_specs, out_specs=P(("slab", "tile"), None), check_vma=False
    )

    def run(*args):
        with jax.sharding.use_abstract_mesh(mesh.abstract_mesh):
            return mapped(*args)

    return run
```

```python
import math

import jax
import jax.numpy as jnp
from jax import lax
from jax.experimental import pallas as pl
from jax.experimental.pallas import tpu as pltpu
from jax.sharding import PartitionSpec as P

EPS = 1e-05
F32 = jnp.float32
BF16 = jnp.bfloat16
I32 = jnp.int32

C = 256
HEADS = 8
HEAD_DIM = 32
PATCH = 1024
ROWS = 2048
RIM = 128
PEERS = 128
CAP = 24
SLOTS = PEERS * CAP
OFFSETS = 27
GROUP = 9
BLOCK = 128
WINDOW = 256
SUPER = 512
QBLOCK = 512
SCORE_SCALE = math.log2(math.e) / math.sqrt(HEAD_DIM)
GELU_A = math.sqrt(2.0 / math.pi)
GELU_B = 0.044715 * GELU_A
VMEM_LIMIT = 60 << 20


def dot(a, b):
    return jnp.dot(a, b, preferred_element_type=F32)


def dot_nt(a, b):
    return lax.dot_general(a, b, (((1,), (1,)), ((), ())), preferred_element_type=F32)


def layer_norm(values, gain):
    centred = values - jnp.mean(values, axis=-1, keepdims=True)
    spread = jnp.mean(centred * centred, axis=-1, keepdims=True)
    return centred * lax.rsqrt(spread + EPS) * gain


def offset(place, base):
    return jnp.clip(place - base, -1, WINDOW).astype(F32).astype(BF16)


def small_iota(shape, axis):
    base = lax.broadcasted_iota(I32, shape, axis)
    return base.astype(F32).astype(BF16)


def hits(place, iota):
    return jnp.where(place == iota, jnp.ones((), BF16), jnp.zeros((), BF16))


def columns(place, count):
    base = jnp.arange(count // WINDOW, dtype=I32) * WINDOW
    return offset(place.reshape(-1, 1), base.reshape(1, -1))


def whole(shape):
    return pl.BlockSpec(shape, lambda i, *_: (0,) * len(shape))


def conv_kernel(
    first_ref, count_ref, own, lower, upper, index, owners, weight_hbm, cpe, gain,
    outgoing, slot, ext, picked_a, picked_b, total, weight, emb, sem,
):
    step = pl.program_id(0)
    blocks = SUPER // BLOCK
    steps = ROWS // SUPER
    fetch = pltpu.make_async_copy(weight_hbm, weight.at[pl.ds(0, OFFSETS * C), :], sem)
    lanes = small_iota((BLOCK, WINDOW), 1)

    @pl.when(step == 0)
    def _():
        fetch.start()
        ext[0:RIM, :] = lower[...]
        ext[RIM : RIM + ROWS, :] = own[...]
        ext[RIM + ROWS : 2 * RIM + ROWS, :] = upper[...]
        ext[2 * RIM + ROWS :, :] = jnp.zeros((WINDOW, C), BF16)
        weight[OFFSETS * C :, :] = jnp.zeros((C, C), BF16)
        picked_a[:, OFFSETS * C :] = jnp.zeros((SUPER, C), BF16)
        picked_b[:, OFFSETS * C :] = jnp.zeros((SUPER, C), BF16)
        total[...] = jnp.zeros((SUPER, C), F32)

    def build(b, picked):
        place = pl.multiple_of(b * BLOCK, BLOCK)
        row = pl.multiple_of(step * SUPER + b * BLOCK, BLOCK)
        columns = jnp.transpose(index[:, pl.ds(row, BLOCK)].astype(F32), (1, 0))

        def window(g, entry, t):
            base = pl.multiple_of(first_ref[entry] + t * WINDOW, 16)
            rels = jnp.clip(columns - base.astype(F32), -1.0, float(WINDOW)).astype(BF16)
            chosen = [hits(rels[:, GROUP * g + k : GROUP * g + k + 1], lanes) for k in range(GROUP)]
            rows = dot(jnp.concatenate(chosen, axis=0), ext[pl.ds(base, WINDOW), :]).astype(BF16)
            return [
                ((pl.ds(place, BLOCK), slice((GROUP * g + k) * C, (GROUP * g + k + 1) * C)), rows[k * BLOCK : (k + 1) * BLOCK, :])
                for k in range(GROUP)
            ]

        groups = [(g, g * (ROWS // BLOCK) + step * blocks + b) for g in range(OFFSETS // GROUP)]
        for g, entry in groups:
            for dst, rows in window(g, entry, 0):
                picked[dst] = rows

        def rest():
            for g, entry in groups:

                def more(t, carry):
                    for dst, rows in window(g, entry, t):
                        picked[dst] = picked[dst] + rows
                    return carry

                lax.fori_loop(1, count_ref[entry], more, 0)

        return rest

    def multiply(b, picked):
        width = (OFFSETS + 1) * C // blocks
        at = pl.multiple_of(b * width, width)
        total[...] += dot(picked[:, pl.ds(at, width)], weight[pl.ds(at, width), :])

    def finish(of):
        at = pl.multiple_of(of * SUPER, SUPER)
        linear = dot(total[...].astype(BF16), cpe[...])
        emb[pl.ds(at, SUPER), :] = (
            own[pl.ds(at, SUPER), :].astype(F32) + layer_norm(linear, gain[...])
        ).astype(BF16)
        total[...] = jnp.zeros((SUPER, C), F32)

    @pl.when(step == 0)
    def _():
        def one_block(b, carry):
            build(b, picked_a)()
            return carry

        lax.fori_loop(0, blocks, one_block, 0)
        fetch.wait()

    for parity, (new, old) in ((1, (picked_b, picked_a)), (0, (picked_a, picked_b))):

        @pl.when((step > 0) & (step < steps) & (lax.rem(step, 2) == parity))
        def _():
            def one_block(b, carry):
                multiply(b, old)
                build(b, new)()
                return carry

            lax.fori_loop(0, blocks, one_block, 0)
            finish(step - 1)

    @pl.when(step == steps)
    def _():
        total[...] = dot(picked_b[...], weight[...])
        finish(step - 1)

    @pl.when(step == steps)
    def _():
        width = 256
        peer = lax.broadcasted_iota(I32, (PEERS, width), 0)
        before = lax.broadcasted_iota(I32, (width, width), 0) < lax.broadcasted_iota(I32, (width, width), 1)
        before = jnp.where(before, 1.0, 0.0).astype(BF16)
        base = jnp.zeros((PEERS, 1), F32)
        for c in range(ROWS // width):
            cols = slice(c * width, (c + 1) * width)
            owner = owners[:, cols]
            mine = jnp.where(peer == owner, 1.0, 0.0)
            seen = dot(mine.astype(BF16), before) + base
            rank = jnp.sum(mine * seen, axis=0, keepdims=True)
            slot[:, cols] = owner * CAP + rank.astype(I32)
            base = base + jnp.sum(mine, axis=1, keepdims=True)
        places = small_iota((WINDOW, ROWS), 0)
        for c in range(SLOTS // WINDOW):
            pick = hits(offset(slot[...], c * WINDOW), places)
            outgoing[c * WINDOW : (c + 1) * WINDOW, :] = dot(pick, emb[...]).astype(BF16)


def conv_part(features, lower, upper, neighbours, validity, owners, conv_weight, cpe_weight, cpe_gain):
    index = jnp.where(validity > 0, neighbours, -1)
    split = (OFFSETS // GROUP, GROUP, ROWS // BLOCK, BLOCK)
    low = jnp.min(jnp.where(validity > 0, neighbours, 2 * ROWS).reshape(split), axis=(1, 3))
    high = jnp.max(index.reshape(split), axis=(1, 3))
    low = jnp.minimum(low, ROWS + 2 * RIM - 1) // 16 * 16
    count = (high - low + WINDOW) // WINDOW
    index = jnp.pad(index, ((0, 5), (0, 0)), constant_values=-1)
    args = (
        features, lower, upper, index, owners.reshape(1, ROWS), conv_weight.reshape(OFFSETS * C, C),
        cpe_weight, cpe_gain.reshape(1, C),
    )
    return pl.pallas_call(
        conv_kernel,
        grid_spec=pltpu.PrefetchScalarGridSpec(
            num_scalar_prefetch=2,
            grid=(ROWS // SUPER + 1,),
            in_specs=[pl.BlockSpec(memory_space=pl.ANY) if i == 5 else whole(a.shape) for i, a in enumerate(args)],
            out_specs=[whole((SLOTS, C)), whole((1, ROWS))],
            scratch_shapes=[
                pltpu.VMEM((ROWS + 2 * RIM + WINDOW, C), BF16),
                pltpu.VMEM((SUPER, (OFFSETS + 1) * C), BF16),
                pltpu.VMEM((SUPER, (OFFSETS + 1) * C), BF16),
                pltpu.VMEM((SUPER, C), F32),
                pltpu.VMEM(((OFFSETS + 1) * C, C), BF16),
                pltpu.VMEM((ROWS, C), BF16),
                pltpu.SemaphoreType.DMA(()),
            ],
        ),
        out_shape=[jax.ShapeDtypeStruct((SLOTS, C), BF16), jax.ShapeDtypeStruct((1, ROWS), I32)],
        compiler_params=pltpu.CompilerParams(vmem_limit_bytes=VMEM_LIMIT),
        name="conv_part",
    )(low.reshape(-1), count.reshape(-1), *args)


def attend_kernel(
    arrived, table_row, table_col, attn_gain, qkv, proj, mlp_gain, up, down,
    leaving, seq, processed, keys, queries, values, mixed, scores_a, scores_b, peak_a, peak_b,
):
    patch = pl.program_id(0)
    places = small_iota((WINDOW, SLOTS), 0)
    for c in range(PATCH // WINDOW):
        rows = slice(c * WINDOW, (c + 1) * WINDOW)
        seq[rows, :] = dot(hits(offset(table_row[...], patch * PATCH + c * WINDOW), places), arrived[...])
    normed = layer_norm(seq[...], attn_gain[...]).astype(BF16)
    queries[...] = dot_nt(jnp.transpose(qkv[:, 0:C], (1, 0)), normed).astype(BF16)
    key_rows = dot(normed, qkv[:, C : 2 * C]).astype(BF16)
    value_cols = dot_nt(jnp.transpose(qkv[:, 2 * C :], (1, 0)), normed).astype(BF16)
    for h in range(HEADS):
        keys[h, :, :] = key_rows[:, HEAD_DIM * h : HEAD_DIM * (h + 1)]
        values[h, 0:HEAD_DIM, :] = value_cols[HEAD_DIM * h : HEAD_DIM * (h + 1), :]
        values[h, HEAD_DIM:, :] = jnp.ones((16, PATCH), BF16)
    per_head = PATCH // QBLOCK
    tasks = HEADS * per_head

    def where_is(t):
        head = lax.div(t, per_head)
        return (
            head,
            pl.multiple_of(head * HEAD_DIM, HEAD_DIM),
            pl.multiple_of(lax.rem(t, per_head) * QBLOCK, QBLOCK),
        )

    def score(t, scores, peak):
        head, row, col = where_is(lax.rem(t, tasks))
        found = dot(keys[head], queries[pl.ds(row, HEAD_DIM), pl.ds(col, QBLOCK)])
        scores[...] = found
        peak[...] = jnp.max(found, axis=0, keepdims=True)

    def mix(t, scores, peak):
        head, row, col = where_is(t)
        raised = jnp.exp2(((scores[...] - peak[...]) * SCORE_SCALE).astype(BF16))
        total = dot(values[head], raised)
        mixed[pl.ds(row, HEAD_DIM), pl.ds(col, QBLOCK)] = total[0:HEAD_DIM, :] / total[HEAD_DIM : HEAD_DIM + 1, :]

    score(0, scores_a, peak_a)

    def one(t, carry):
        @pl.when(lax.rem(t, 2) == 0)
        def _():
            score(t + 1, scores_b, peak_b)
            mix(t, scores_a, peak_a)

        @pl.when(lax.rem(t, 2) == 1)
        def _():
            score(t + 1, scores_a, peak_a)
            mix(t, scores_b, peak_b)

        return carry

    lax.fori_loop(0, tasks, one, 0)
    attended = jnp.transpose(mixed[...], (1, 0)).astype(BF16)
    after = (seq[...] + dot(attended, proj[...])).astype(BF16).astype(F32)
    normed_two = layer_norm(after, mlp_gain[...]).astype(BF16)
    wide = dot(normed_two, up[...])
    inner = wide * (GELU_A + GELU_B * (wide * wide))
    hidden = (wide + wide * jnp.tanh(inner)).astype(BF16)
    at = pl.multiple_of(patch * PATCH, PATCH)
    processed[pl.ds(at, PATCH), :] = (after + 0.5 * dot(hidden, down[...])).astype(BF16)

    @pl.when(patch == ROWS // PATCH - 1)
    def _():
        chunk = 512
        lanes = small_iota((chunk, WINDOW), 1)
        for c in range(SLOTS // chunk):
            rows = slice(c * chunk, (c + 1) * chunk)
            pick = [hits(table_col[rows, w : w + 1], lanes) for w in range(ROWS // WINDOW)]
            leaving[rows, :] = dot(jnp.concatenate(pick, axis=1), processed[...]).astype(BF16)


def attend_part(arrived, slot_table, attn_gain, qkv_weight, proj_weight, mlp_gain, mlp_up, mlp_down):
    args = (
        arrived, slot_table.reshape(1, SLOTS), columns(slot_table, ROWS), attn_gain.reshape(1, C),
        qkv_weight, proj_weight, mlp_gain.reshape(1, C), mlp_up, mlp_down,
    )
    return pl.pallas_call(
        attend_kernel,
        grid=(ROWS // PATCH,),
        in_specs=[whole(a.shape) for a in args],
        out_specs=whole((SLOTS, C)),
        out_shape=jax.ShapeDtypeStruct((SLOTS, C), BF16),
        scratch_shapes=[
            pltpu.VMEM((PATCH, C), F32),
            pltpu.VMEM((ROWS, C), BF16),
            pltpu.VMEM((HEADS, PATCH, HEAD_DIM), BF16),
            pltpu.VMEM((C, PATCH), BF16),
            pltpu.VMEM((HEADS, HEAD_DIM + 16, PATCH), BF16),
            pltpu.VMEM((C, PATCH), F32),
            pltpu.VMEM((PATCH, QBLOCK), F32),
            pltpu.VMEM((PATCH, QBLOCK), F32),
            pltpu.VMEM((1, QBLOCK), F32),
            pltpu.VMEM((1, QBLOCK), F32),
        ],
        compiler_params=pltpu.CompilerParams(vmem_limit_bytes=VMEM_LIMIT),
        name="attend_part",
    )(*args)


def return_kernel(returned, slot_col, out):
    lanes = small_iota((out.shape[0], WINDOW), 1)
    pick = [hits(slot_col[:, w : w + 1], lanes) for w in range(SLOTS // WINDOW)]
    out[...] = dot(jnp.concatenate(pick, axis=1), returned[...]).astype(BF16)


def return_part(returned, slot):
    rows = 512
    return pl.pallas_call(
        return_kernel,
        grid=(ROWS // rows,),
        in_specs=[whole((SLOTS, C)), pl.BlockSpec((rows, SLOTS // WINDOW), lambda i: (i, 0))],
        out_specs=pl.BlockSpec((rows, C), lambda i: (i, 0)),
        out_shape=jax.ShapeDtypeStruct((ROWS, C), BF16),
        compiler_params=pltpu.CompilerParams(vmem_limit_bytes=VMEM_LIMIT),
        name="return_part",
    )(returned, columns(slot, SLOTS))


def exchange(rows):
    return lax.all_to_all(
        rows.reshape(PEERS, CAP, C), ("slab", "tile"), split_axis=0, concat_axis=0, tiled=True
    ).reshape(SLOTS, C)


def local(
    features, neighbours, validity, owners, slot_table, conv_weight, cpe_weight, cpe_gain,
    attn_gain, qkv_weight, proj_weight, mlp_gain, mlp_up, mlp_down,
):
    slabs = lax.axis_size("slab")
    lower = lax.ppermute(features[ROWS - RIM :], "slab", [(i, i + 1) for i in range(slabs - 1)])
    upper = lax.ppermute(features[:RIM], "slab", [(i + 1, i) for i in range(slabs - 1)])
    outgoing, slot = conv_part(
        features, lower, upper, neighbours, validity, owners, conv_weight, cpe_weight, cpe_gain
    )
    leaving = attend_part(
        exchange(outgoing), slot_table, attn_gain, qkv_weight, proj_weight, mlp_gain, mlp_up, mlp_down
    )
    return return_part(exchange(leaving), slot)


def solution(mesh):
    both = P(("slab", "tile"))
    in_specs = (
        P(("slab", "tile"), None), P(None, ("slab", "tile")), P(None, ("slab", "tile")), both, both,
    ) + (P(),) * 9
    mapped = jax.shard_map(
        local, mesh=mesh, in_specs=in_specs, out_specs=P(("slab", "tile"), None), check_vma=False
    )

    def run(*args):
        with jax.sharding.use_abstract_mesh(mesh.abstract_mesh):
            return mapped(*args)

    return run
```

```python
import math

import jax
import jax.numpy as jnp
from jax import lax
from jax.experimental import pallas as pl
from jax.experimental.pallas import tpu as pltpu
from jax.sharding import PartitionSpec as P

EPS = 1e-05
F32 = jnp.float32
BF16 = jnp.bfloat16
I32 = jnp.int32

C = 256
HEADS = 8
HEAD_DIM = 32
PATCH = 1024
ROWS = 2048
RIM = 128
PEERS = 128
CAP = 24
SLOTS = PEERS * CAP
OFFSETS = 27
GROUP = 9
BLOCK = 128
WINDOW = 256
SUPER = 1024
TOGETHER = 4
OUT_CHUNK = 768
SEQ_CHUNK = 256
LEAVE_CHUNK = 512
RETURN_ROWS = 1024
QBLOCK = 512
SCORE_SCALE = math.log2(math.e) / math.sqrt(HEAD_DIM)
GELU_A = math.sqrt(2.0 / math.pi)
GELU_B = 0.044715 * GELU_A


def dot(a, b):
    return jnp.dot(a, b, preferred_element_type=F32)


def dot_nt(a, b):
    return lax.dot_general(a, b, (((1,), (1,)), ((), ())), preferred_element_type=F32)


def layer_norm(values, gain):
    centred = values - jnp.mean(values, axis=-1, keepdims=True)
    spread = jnp.mean(centred * centred, axis=-1, keepdims=True)
    return centred * lax.rsqrt(spread + EPS) * gain


def offset(place, base):
    return jnp.clip(place - base, -1, WINDOW).astype(F32).astype(BF16)


def small_iota(shape, axis):
    base = lax.broadcasted_iota(I32, shape, axis)
    return base.astype(F32).astype(BF16)


def hits(place, iota):
    return jnp.where(place == iota, jnp.ones((), BF16), jnp.zeros((), BF16))


def columns(place, count):
    base = jnp.arange(count // WINDOW, dtype=I32) * WINDOW
    return offset(place.reshape(-1, 1), base.reshape(1, -1))


def near(array):
    return pltpu.with_memory_space_constraint(array, pltpu.VMEM)


def whole(shape):
    return pl.BlockSpec(shape, lambda i, *_: (0,) * len(shape))


def conv_kernel(
    first_ref, count_ref, most_ref, own, lower, upper, index, owners, weight_hbm, cpe, gain,
    outgoing, slot, ext, picked, weight, emb, sem,
):
    fetch = pltpu.make_async_copy(weight_hbm, weight, sem)
    fetch.start()
    ext[0:RIM, :] = lower[...]
    ext[RIM : RIM + ROWS, :] = own[...]
    ext[RIM + ROWS : 2 * RIM + ROWS, :] = upper[...]
    ext[2 * RIM + ROWS :, :] = jnp.zeros((WINDOW, C), BF16)
    lanes = small_iota((BLOCK, WINDOW), 1)

    def place(b):
        row = pl.multiple_of(b * BLOCK, BLOCK)
        return row, jnp.transpose(index[:, pl.ds(row, BLOCK)].astype(F32), (1, 0))

    def window(row, columns, g, entry, t):
        base = pl.multiple_of(first_ref[entry] + t * WINDOW, 16)
        rels = jnp.clip(columns - base.astype(F32), -1.0, float(WINDOW)).astype(BF16)
        chosen = [hits(rels[:, GROUP * g + k : GROUP * g + k + 1], lanes) for k in range(GROUP)]
        rows = dot(jnp.concatenate(chosen, axis=0), ext[pl.ds(base, WINDOW), :]).astype(BF16)
        return [
            ((pl.ds(row, BLOCK), slice((GROUP * g + k) * C, (GROUP * g + k + 1) * C)), rows[k * BLOCK : (k + 1) * BLOCK, :])
            for k in range(GROUP)
        ]

    def build(b):
        row, columns = place(b)
        for g in range(OFFSETS // GROUP):
            for dst, rows in window(row, columns, g, g * (ROWS // BLOCK) + b, 0):
                picked[dst] = rows

    def build_rest(b, carry):
        row, columns = place(b)
        for g in range(OFFSETS // GROUP):

            def more(t, carry):
                for dst, rows in window(row, columns, g, g * (ROWS // BLOCK) + b, t):
                    picked[dst] = picked[dst] + rows
                return carry

            lax.fori_loop(1, count_ref[g * (ROWS // BLOCK) + b], more, 0)
        return carry

    def some_blocks(i, carry):
        for j in range(TOGETHER):
            build(i * TOGETHER + j)
        return carry

    lax.fori_loop(0, ROWS // BLOCK // TOGETHER, some_blocks, 0)

    @pl.when(most_ref[0] > 1)
    def _():
        lax.fori_loop(0, ROWS // BLOCK, build_rest, 0)

    fetch.wait()

    width = 256
    peer = lax.broadcasted_iota(I32, (PEERS, width), 0)
    before = lax.broadcasted_iota(I32, (width, width), 0) < lax.broadcasted_iota(I32, (width, width), 1)
    before = jnp.where(before, 1.0, 0.0).astype(BF16)
    base = jnp.zeros((PEERS, 1), F32)
    for c in range(ROWS // width):
        cols = slice(c * width, (c + 1) * width)
        owner = owners[:, cols]
        mine = jnp.where(peer == owner, 1.0, 0.0)
        seen = dot(mine.astype(BF16), before) + base
        rank = jnp.sum(mine * seen, axis=0, keepdims=True)
        slot[:, cols] = owner * CAP + rank.astype(I32)
        base = base + jnp.sum(mine, axis=1, keepdims=True)

    for c in range(ROWS // SUPER):
        rows = slice(c * SUPER, (c + 1) * SUPER)
        linear = dot(dot(picked[rows, :], weight[...]).astype(BF16), cpe[...])
        emb[rows, :] = (own[rows, :].astype(F32) + layer_norm(linear, gain[...])).astype(BF16)

    places = small_iota((WINDOW, ROWS), 0)
    for c in range(SLOTS // OUT_CHUNK):
        at = (c % 2) * OUT_CHUNK
        for w in range(OUT_CHUNK // WINDOW):
            picked[at + w * WINDOW : at + (w + 1) * WINDOW, 0:ROWS] = hits(offset(slot[...], c * OUT_CHUNK + w * WINDOW), places)
        outgoing[c * OUT_CHUNK : (c + 1) * OUT_CHUNK, :] = dot(picked[at : at + OUT_CHUNK, 0:ROWS], emb[...]).astype(BF16)


def conv_part(features, lower, upper, neighbours, validity, owners, conv_weight, cpe_weight, cpe_gain):
    index = jnp.where(validity > 0, neighbours, -1)
    split = (OFFSETS // GROUP, GROUP, ROWS // BLOCK, BLOCK)
    low = jnp.min(jnp.where(validity > 0, neighbours, 2 * ROWS).reshape(split), axis=(1, 3))
    high = jnp.max(index.reshape(split), axis=(1, 3))
    low = jnp.minimum(low, ROWS + 2 * RIM - 1) // 16 * 16
    count = (high - low + WINDOW) // WINDOW
    index = jnp.pad(index, ((0, 5), (0, 0)), constant_values=-1)
    args = (
        low.reshape(-1), count.reshape(-1), jnp.max(count).reshape(1), features, lower, upper, index, owners.reshape(1, ROWS),
        conv_weight.reshape(OFFSETS * C, C), cpe_weight, cpe_gain.reshape(1, C),
    )
    spaces = [pltpu.SMEM] * 3 + [pltpu.VMEM] * 5 + [pl.ANY] + [pltpu.VMEM] * 2
    return pl.pallas_call(
        conv_kernel,
        in_specs=[pl.BlockSpec(memory_space=m) for m in spaces],
        out_specs=[pl.BlockSpec(memory_space=pltpu.VMEM)] * 2,
        scratch_shapes=[
            pltpu.VMEM((ROWS + 2 * RIM + WINDOW, C), BF16),
            pltpu.VMEM((ROWS, OFFSETS * C), BF16),
            pltpu.VMEM((OFFSETS * C, C), BF16),
            pltpu.VMEM((ROWS, C), BF16),
            pltpu.SemaphoreType.DMA(()),
        ],
        out_shape=[jax.ShapeDtypeStruct((SLOTS, C), BF16), jax.ShapeDtypeStruct((1, ROWS), I32)],
        compiler_params=pltpu.CompilerParams(vmem_limit_bytes=46 << 20),
        name="conv_part",
    )(*args)


def attend_kernel(
    arrived, table_row, table_col, attn_gain, qkv, proj, mlp_gain, up, down,
    leaving, seq, processed, keys, queries, values, mixed, scores_a, scores_b, peak_a, peak_b,
):
    patch = pl.program_id(0)
    places = small_iota((WINDOW, SLOTS), 0)
    for c in range(PATCH // SEQ_CHUNK):
        rows = slice(c * SEQ_CHUNK, (c + 1) * SEQ_CHUNK)
        pick = [
            hits(offset(table_row[...], patch * PATCH + c * SEQ_CHUNK + w), places) for w in range(0, SEQ_CHUNK, WINDOW)
        ]
        seq[rows, :] = dot(jnp.concatenate(pick, axis=0), arrived[...])
    normed = layer_norm(seq[...], attn_gain[...]).astype(BF16)
    queries[...] = dot_nt(jnp.transpose(qkv[:, 0:C], (1, 0)), normed).astype(BF16)
    key_rows = dot(normed, qkv[:, C : 2 * C]).astype(BF16)
    value_cols = dot_nt(jnp.transpose(qkv[:, 2 * C :], (1, 0)), normed).astype(BF16)
    for h in range(HEADS):
        keys[h, :, :] = key_rows[:, HEAD_DIM * h : HEAD_DIM * (h + 1)]
        values[h, 0:HEAD_DIM, :] = value_cols[HEAD_DIM * h : HEAD_DIM * (h + 1), :]
        values[h, HEAD_DIM:, :] = jnp.ones((16, PATCH), BF16)
    per_head = PATCH // QBLOCK
    tasks = HEADS * per_head

    def where_is(t):
        head = lax.div(t, per_head)
        return (
            head,
            pl.multiple_of(head * HEAD_DIM, HEAD_DIM),
            pl.multiple_of(lax.rem(t, per_head) * QBLOCK, QBLOCK),
        )

    def score(t, scores, peak):
        head, row, col = where_is(lax.rem(t, tasks))
        found = dot(keys[head], queries[pl.ds(row, HEAD_DIM), pl.ds(col, QBLOCK)])
        scores[...] = found
        peak[...] = jnp.max(found, axis=0, keepdims=True)

    def mix(t, scores, peak):
        head, row, col = where_is(t)
        raised = jnp.exp2(((scores[...] - peak[...]) * SCORE_SCALE).astype(BF16))
        total = dot(values[head], raised)
        mixed[pl.ds(row, HEAD_DIM), pl.ds(col, QBLOCK)] = total[0:HEAD_DIM, :] / total[HEAD_DIM : HEAD_DIM + 1, :]

    score(0, scores_a, peak_a)

    def one(t, carry):
        @pl.when(lax.rem(t, 2) == 0)
        def _():
            score(t + 1, scores_b, peak_b)
            mix(t, scores_a, peak_a)

        @pl.when(lax.rem(t, 2) == 1)
        def _():
            score(t + 1, scores_a, peak_a)
            mix(t, scores_b, peak_b)

        return carry

    lax.fori_loop(0, tasks, one, 0)
    attended = jnp.transpose(mixed[...], (1, 0)).astype(BF16)
    after = (seq[...] + dot(attended, proj[...])).astype(BF16).astype(F32)
    normed_two = layer_norm(after, mlp_gain[...]).astype(BF16)
    wide = dot(normed_two, up[...])
    inner = wide * (GELU_A + GELU_B * (wide * wide))
    hidden = (wide + wide * jnp.tanh(inner)).astype(BF16)
    at = pl.multiple_of(patch * PATCH, PATCH)
    processed[pl.ds(at, PATCH), :] = (after + 0.5 * dot(hidden, down[...])).astype(BF16)

    @pl.when(patch == ROWS // PATCH - 1)
    def _():
        chunk = LEAVE_CHUNK
        lanes = small_iota((chunk, WINDOW), 1)
        for c in range(SLOTS // chunk):
            rows = slice(c * chunk, (c + 1) * chunk)
            pick = [hits(table_col[rows, w : w + 1], lanes) for w in range(ROWS // WINDOW)]
            leaving[rows, :] = dot(jnp.concatenate(pick, axis=1), processed[...]).astype(BF16)


def attend_part(arrived, slot_table, attn_gain, qkv_weight, proj_weight, mlp_gain, mlp_up, mlp_down):
    args = (
        arrived, slot_table.reshape(1, SLOTS), near(columns(slot_table, ROWS)), attn_gain.reshape(1, C),
        near(qkv_weight), near(proj_weight), mlp_gain.reshape(1, C), near(mlp_up), near(mlp_down),
    )
    return pl.pallas_call(
        attend_kernel,
        grid=(ROWS // PATCH,),
        in_specs=[pl.BlockSpec(memory_space=pltpu.VMEM) for a in args],
        out_specs=pl.BlockSpec(memory_space=pltpu.VMEM),
        out_shape=jax.ShapeDtypeStruct((SLOTS, C), BF16),
        scratch_shapes=[
            pltpu.VMEM((PATCH, C), F32),
            pltpu.VMEM((ROWS, C), BF16),
            pltpu.VMEM((HEADS, PATCH, HEAD_DIM), BF16),
            pltpu.VMEM((C, PATCH), BF16),
            pltpu.VMEM((HEADS, HEAD_DIM + 16, PATCH), BF16),
            pltpu.VMEM((C, PATCH), F32),
            pltpu.VMEM((PATCH, QBLOCK), F32),
            pltpu.VMEM((PATCH, QBLOCK), F32),
            pltpu.VMEM((1, QBLOCK), F32),
            pltpu.VMEM((1, QBLOCK), F32),
        ],
        compiler_params=pltpu.CompilerParams(vmem_limit_bytes=36 << 20),
        name="attend_part",
    )(*args)


def return_kernel(returned, slot_col, out):
    count = out.shape[0]
    lanes = small_iota((count, WINDOW), 1)
    rows = pl.ds(pl.multiple_of(pl.program_id(0) * count, count), count)
    pick = [hits(slot_col[rows, w : w + 1], lanes) for w in range(SLOTS // WINDOW)]
    out[...] = dot(jnp.concatenate(pick, axis=1), returned[...]).astype(BF16)


def return_part(returned, slot):
    rows = RETURN_ROWS
    return pl.pallas_call(
        return_kernel,
        grid=(ROWS // rows,),
        in_specs=[pl.BlockSpec(memory_space=pltpu.VMEM)] * 2,
        out_specs=pl.BlockSpec((rows, C), lambda i: (i, 0)),
        out_shape=jax.ShapeDtypeStruct((ROWS, C), BF16),
        compiler_params=pltpu.CompilerParams(vmem_limit_bytes=24 << 20),
        name="return_part",
    )(returned, near(columns(slot, SLOTS)))


def exchange(rows):
    rows = lax.all_to_all(
        rows.reshape(PEERS, CAP, C), ("slab", "tile"), split_axis=0, concat_axis=0, tiled=True
    ).reshape(SLOTS, C)
    return near(rows)


def local(
    features, neighbours, validity, owners, slot_table, conv_weight, cpe_weight, cpe_gain,
    attn_gain, qkv_weight, proj_weight, mlp_gain, mlp_up, mlp_down,
):
    slabs = lax.axis_size("slab")
    lower = lax.ppermute(features[ROWS - RIM :], "slab", [(i, i + 1) for i in range(slabs - 1)])
    upper = lax.ppermute(features[:RIM], "slab", [(i + 1, i) for i in range(slabs - 1)])
    outgoing, slot = conv_part(
        features, lower, upper, neighbours, validity, owners, conv_weight, cpe_weight, cpe_gain
    )
    leaving = attend_part(
        exchange(outgoing), slot_table, attn_gain, qkv_weight, proj_weight, mlp_gain, mlp_up, mlp_down
    )
    return return_part(exchange(leaving), slot)


def solution(mesh):
    both = P(("slab", "tile"))
    in_specs = (
        P(("slab", "tile"), None), P(None, ("slab", "tile")), P(None, ("slab", "tile")), both, both,
    ) + (P(),) * 9
    mapped = jax.shard_map(
        local, mesh=mesh, in_specs=in_specs, out_specs=P(("slab", "tile"), None), check_vma=False
    )

    def run(*args):
        with jax.sharding.use_abstract_mesh(mesh.abstract_mesh):
            return mapped(*args)

    return run
```

```python
import math

import jax
import jax.numpy as jnp
from jax import lax
from jax.experimental import pallas as pl
from jax.experimental.pallas import tpu as pltpu
from jax.sharding import PartitionSpec as P

EPS = 1e-05
F32 = jnp.float32
BF16 = jnp.bfloat16
I32 = jnp.int32

C = 256
HEADS = 8
HEAD_DIM = 32
PATCH = 1024
ROWS = 2048
RIM = 128
PEERS = 128
CAP = 24
SLOTS = PEERS * CAP
OFFSETS = 27
GROUP = 9
BLOCK = 128
WINDOW = 256
SUPER = 1024
TOGETHER = 4
OUT_CHUNK = 768
SEQ_CHUNK = 256
LEAVE_CHUNK = 512
RETURN_ROWS = 1024
QBLOCK = 512
SCORE_SCALE = math.log2(math.e) / math.sqrt(HEAD_DIM)
GELU_A = math.sqrt(2.0 / math.pi)
GELU_B = 0.044715 * GELU_A


def dot(a, b):
    return jnp.dot(a, b, preferred_element_type=F32)


def dot_nt(a, b):
    return lax.dot_general(a, b, (((1,), (1,)), ((), ())), preferred_element_type=F32)


def layer_norm(values, gain):
    centred = values - jnp.mean(values, axis=-1, keepdims=True)
    spread = jnp.mean(centred * centred, axis=-1, keepdims=True)
    return centred * lax.rsqrt(spread + EPS) * gain


def offset(place, base):
    return jnp.clip(place - base, -1, WINDOW).astype(F32).astype(BF16)


def small_iota(shape, axis):
    base = lax.broadcasted_iota(I32, shape, axis)
    return base.astype(F32).astype(BF16)


def hits(place, iota):
    return jnp.where(place == iota, jnp.ones((), BF16), jnp.zeros((), BF16))


def columns(place, count):
    base = jnp.arange(count // WINDOW, dtype=I32) * WINDOW
    return offset(place.reshape(-1, 1), base.reshape(1, -1))


def near(array):
    return pltpu.with_memory_space_constraint(array, pltpu.VMEM)


def whole(shape):
    return pl.BlockSpec(shape, lambda i, *_: (0,) * len(shape))


def conv_kernel(
    first_ref, count_ref, most_ref, own, lower, upper, index, valid, owners, weight_hbm, cpe, gain,
    outgoing, slot, ext, picked, weight, emb, sem,
):
    fetch = pltpu.make_async_copy(weight_hbm, weight, sem)
    fetch.start()
    ext[0:RIM, :] = lower[...]
    ext[RIM : RIM + ROWS, :] = own[...]
    ext[RIM + ROWS : 2 * RIM + ROWS, :] = upper[...]
    ext[2 * RIM + ROWS :, :] = jnp.zeros((WINDOW, C), BF16)
    lanes = small_iota((BLOCK, WINDOW), 1)

    def place(b):
        row = pl.multiple_of(b * BLOCK, BLOCK)
        cols = pl.ds(row, BLOCK)
        return row, jnp.transpose(jnp.where(valid[:, cols] > 0, index[:, cols], -1).astype(F32), (1, 0))

    def window(row, columns, g, entry, t):
        base = pl.multiple_of(first_ref[entry] + t * WINDOW, 16)
        rels = jnp.clip(columns - base.astype(F32), -1.0, float(WINDOW)).astype(BF16)
        chosen = [hits(rels[:, GROUP * g + k : GROUP * g + k + 1], lanes) for k in range(GROUP)]
        rows = dot(jnp.concatenate(chosen, axis=0), ext[pl.ds(base, WINDOW), :]).astype(BF16)
        return [
            ((pl.ds(row, BLOCK), slice((GROUP * g + k) * C, (GROUP * g + k + 1) * C)), rows[k * BLOCK : (k + 1) * BLOCK, :])
            for k in range(GROUP)
        ]

    def build(b):
        row, columns = place(b)
        for g in range(OFFSETS // GROUP):
            for dst, rows in window(row, columns, g, g * (ROWS // BLOCK) + b, 0):
                picked[dst] = rows

    def build_rest(b, carry):
        row, columns = place(b)
        for g in range(OFFSETS // GROUP):

            def more(t, carry):
                for dst, rows in window(row, columns, g, g * (ROWS // BLOCK) + b, t):
                    picked[dst] = picked[dst] + rows
                return carry

            lax.fori_loop(1, count_ref[g * (ROWS // BLOCK) + b], more, 0)
        return carry

    def some_blocks(i, carry):
        for j in range(TOGETHER):
            build(i * TOGETHER + j)
        return carry

    lax.fori_loop(0, ROWS // BLOCK // TOGETHER, some_blocks, 0)

    @pl.when(most_ref[0] > 1)
    def _():
        lax.fori_loop(0, ROWS // BLOCK, build_rest, 0)

    fetch.wait()

    width = 256
    peer = lax.broadcasted_iota(I32, (PEERS, width), 0)
    before = lax.broadcasted_iota(I32, (width, width), 0) < lax.broadcasted_iota(I32, (width, width), 1)
    before = jnp.where(before, 1.0, 0.0).astype(BF16)
    base = jnp.zeros((PEERS, 1), F32)
    for c in range(ROWS // width):
        cols = slice(c * width, (c + 1) * width)
        owner = owners[:, cols]
        mine = jnp.where(peer == owner, 1.0, 0.0)
        seen = dot(mine.astype(BF16), before) + base
        rank = jnp.sum(mine * seen, axis=0, keepdims=True)
        slot[:, cols] = owner * CAP + rank.astype(I32)
        base = base + jnp.sum(mine, axis=1, keepdims=True)

    for c in range(ROWS // SUPER):
        rows = slice(c * SUPER, (c + 1) * SUPER)
        linear = dot(dot(picked[rows, :], weight[...]).astype(BF16), cpe[...])
        emb[rows, :] = (own[rows, :].astype(F32) + layer_norm(linear, gain[...])).astype(BF16)

    places = small_iota((WINDOW, ROWS), 0)
    for c in range(SLOTS // OUT_CHUNK):
        at = (c % 2) * OUT_CHUNK
        for w in range(OUT_CHUNK // WINDOW):
            picked[at + w * WINDOW : at + (w + 1) * WINDOW, 0:ROWS] = hits(offset(slot[...], c * OUT_CHUNK + w * WINDOW), places)
        outgoing[c * OUT_CHUNK : (c + 1) * OUT_CHUNK, :] = dot(picked[at : at + OUT_CHUNK, 0:ROWS], emb[...]).astype(BF16)


def conv_part(features, lower, upper, neighbours, validity, owners, conv_weight, cpe_weight, cpe_gain):
    index = jnp.where(validity > 0, neighbours, -1)
    split = (OFFSETS // GROUP, GROUP, ROWS // BLOCK, BLOCK)
    low = jnp.min(jnp.where(validity > 0, neighbours, 2 * ROWS).reshape(split), axis=(1, 3))
    high = jnp.max(index.reshape(split), axis=(1, 3))
    low = jnp.minimum(low, ROWS + 2 * RIM - 1) & -16
    count = (high - low + WINDOW) >> 8
    args = (
        low.reshape(-1), count.reshape(-1), jnp.max(count).reshape(1), features, lower, upper, neighbours, validity, owners.reshape(1, ROWS),
        conv_weight.reshape(OFFSETS * C, C), cpe_weight, cpe_gain.reshape(1, C),
    )
    spaces = [pltpu.SMEM] * 3 + [pltpu.VMEM] * 6 + [pl.ANY] + [pltpu.VMEM] * 2
    return pl.pallas_call(
        conv_kernel,
        in_specs=[pl.BlockSpec(memory_space=m) for m in spaces],
        out_specs=[pl.BlockSpec(memory_space=pltpu.VMEM)] * 2,
        scratch_shapes=[
            pltpu.VMEM((ROWS + 2 * RIM + WINDOW, C), BF16),
            pltpu.VMEM((ROWS, OFFSETS * C), BF16),
            pltpu.VMEM((OFFSETS * C, C), BF16),
            pltpu.VMEM((ROWS, C), BF16),
            pltpu.SemaphoreType.DMA(()),
        ],
        out_shape=[jax.ShapeDtypeStruct((SLOTS, C), BF16), jax.ShapeDtypeStruct((1, ROWS), I32)],
        compiler_params=pltpu.CompilerParams(vmem_limit_bytes=52 << 20),
        name="conv_part",
    )(*args)


def attend_kernel(
    arrived, table_row, table_col, attn_gain, qkv, proj, mlp_gain, up, down,
    leaving, seq, processed, keys, queries, values, mixed, scores_a, scores_b, peak_a, peak_b,
):
    patch = pl.program_id(0)
    places = small_iota((WINDOW, SLOTS), 0)
    for c in range(PATCH // SEQ_CHUNK):
        rows = slice(c * SEQ_CHUNK, (c + 1) * SEQ_CHUNK)
        pick = [
            hits(offset(table_row[...], patch * PATCH + c * SEQ_CHUNK + w), places) for w in range(0, SEQ_CHUNK, WINDOW)
        ]
        seq[rows, :] = dot(jnp.concatenate(pick, axis=0), arrived[...])
    normed = layer_norm(seq[...], attn_gain[...]).astype(BF16)
    queries[...] = dot_nt(jnp.transpose(qkv[:, 0:C], (1, 0)), normed).astype(BF16)
    key_rows = dot(normed, qkv[:, C : 2 * C]).astype(BF16)
    value_cols = dot_nt(jnp.transpose(qkv[:, 2 * C :], (1, 0)), normed).astype(BF16)
    for h in range(HEADS):
        keys[h, :, :] = key_rows[:, HEAD_DIM * h : HEAD_DIM * (h + 1)]
        values[h, 0:HEAD_DIM, :] = value_cols[HEAD_DIM * h : HEAD_DIM * (h + 1), :]
        values[h, HEAD_DIM:, :] = jnp.ones((16, PATCH), BF16)
    per_head = PATCH // QBLOCK
    tasks = HEADS * per_head

    def where_is(t):
        head = lax.div(t, per_head)
        return (
            head,
            pl.multiple_of(head * HEAD_DIM, HEAD_DIM),
            pl.multiple_of(lax.rem(t, per_head) * QBLOCK, QBLOCK),
        )

    def score(t, scores, peak):
        head, row, col = where_is(lax.rem(t, tasks))
        found = dot(keys[head], queries[pl.ds(row, HEAD_DIM), pl.ds(col, QBLOCK)])
        scores[...] = found
        peak[...] = jnp.max(found, axis=0, keepdims=True)

    def mix(t, scores, peak):
        head, row, col = where_is(t)
        raised = jnp.exp2(((scores[...] - peak[...]) * SCORE_SCALE).astype(BF16))
        total = dot(values[head], raised)
        mixed[pl.ds(row, HEAD_DIM), pl.ds(col, QBLOCK)] = total[0:HEAD_DIM, :] / total[HEAD_DIM : HEAD_DIM + 1, :]

    score(0, scores_a, peak_a)

    def one(t, carry):
        @pl.when(lax.rem(t, 2) == 0)
        def _():
            score(t + 1, scores_b, peak_b)
            mix(t, scores_a, peak_a)

        @pl.when(lax.rem(t, 2) == 1)
        def _():
            score(t + 1, scores_a, peak_a)
            mix(t, scores_b, peak_b)

        return carry

    lax.fori_loop(0, tasks, one, 0)
    attended = jnp.transpose(mixed[...], (1, 0)).astype(BF16)
    after = (seq[...] + dot(attended, proj[...])).astype(BF16).astype(F32)
    normed_two = layer_norm(after, mlp_gain[...]).astype(BF16)
    wide = dot(normed_two, up[...])
    inner = wide * (GELU_A + GELU_B * (wide * wide))
    hidden = (wide + wide * jnp.tanh(inner)).astype(BF16)
    at = pl.multiple_of(patch * PATCH, PATCH)
    processed[pl.ds(at, PATCH), :] = (after + 0.5 * dot(hidden, down[...])).astype(BF16)

    @pl.when(patch == ROWS // PATCH - 1)
    def _():
        chunk = LEAVE_CHUNK
        lanes = small_iota((chunk, WINDOW), 1)
        for c in range(SLOTS // chunk):
            rows = slice(c * chunk, (c + 1) * chunk)
            pick = [hits(table_col[rows, w : w + 1], lanes) for w in range(ROWS // WINDOW)]
            leaving[rows, :] = dot(jnp.concatenate(pick, axis=1), processed[...]).astype(BF16)


def attend_part(arrived, slot_table, attn_gain, qkv_weight, proj_weight, mlp_gain, mlp_up, mlp_down):
    args = (
        arrived, slot_table.reshape(1, SLOTS), near(columns(slot_table, ROWS)), attn_gain.reshape(1, C),
        qkv_weight, proj_weight, mlp_gain.reshape(1, C), mlp_up, mlp_down,
    )
    return pl.pallas_call(
        attend_kernel,
        grid=(ROWS // PATCH,),
        in_specs=[pl.BlockSpec(memory_space=pltpu.VMEM) for a in args],
        out_specs=pl.BlockSpec(memory_space=pltpu.VMEM),
        out_shape=jax.ShapeDtypeStruct((SLOTS, C), BF16),
        scratch_shapes=[
            pltpu.VMEM((PATCH, C), F32),
            pltpu.VMEM((ROWS, C), BF16),
            pltpu.VMEM((HEADS, PATCH, HEAD_DIM), BF16),
            pltpu.VMEM((C, PATCH), BF16),
            pltpu.VMEM((HEADS, HEAD_DIM + 16, PATCH), BF16),
            pltpu.VMEM((C, PATCH), F32),
            pltpu.VMEM((PATCH, QBLOCK), F32),
            pltpu.VMEM((PATCH, QBLOCK), F32),
            pltpu.VMEM((1, QBLOCK), F32),
            pltpu.VMEM((1, QBLOCK), F32),
        ],
        compiler_params=pltpu.CompilerParams(vmem_limit_bytes=52 << 20),
        name="attend_part",
    )(*args)


def return_kernel(returned, slot_col, out):
    count = out.shape[0]
    lanes = small_iota((count, WINDOW), 1)
    rows = pl.ds(pl.multiple_of(pl.program_id(0) * count, count), count)
    pick = [hits(slot_col[rows, w : w + 1], lanes) for w in range(SLOTS // WINDOW)]
    out[...] = dot(jnp.concatenate(pick, axis=1), returned[...]).astype(BF16)


def return_part(returned, slot):
    rows = RETURN_ROWS
    return pl.pallas_call(
        return_kernel,
        grid=(ROWS // rows,),
        in_specs=[pl.BlockSpec(memory_space=pltpu.VMEM)] * 2,
        out_specs=pl.BlockSpec((rows, C), lambda i: (i, 0)),
        out_shape=jax.ShapeDtypeStruct((ROWS, C), BF16),
        compiler_params=pltpu.CompilerParams(vmem_limit_bytes=52 << 20),
        name="return_part",
    )(returned, near(columns(slot, SLOTS)))


def exchange(rows):
    rows = lax.all_to_all(
        rows.reshape(PEERS, CAP, C), ("slab", "tile"), split_axis=0, concat_axis=0, tiled=True
    ).reshape(SLOTS, C)
    return near(rows)


def local(
    features, neighbours, validity, owners, slot_table, conv_weight, cpe_weight, cpe_gain,
    attn_gain, qkv_weight, proj_weight, mlp_gain, mlp_up, mlp_down,
):
    slabs = lax.axis_size("slab")
    lower = lax.ppermute(features[ROWS - RIM :], "slab", [(i, i + 1) for i in range(slabs - 1)])
    upper = lax.ppermute(features[:RIM], "slab", [(i + 1, i) for i in range(slabs - 1)])
    outgoing, slot = conv_part(
        features, lower, upper, neighbours, validity, owners, conv_weight, cpe_weight, cpe_gain
    )
    leaving = attend_part(
        exchange(outgoing), slot_table, attn_gain, qkv_weight, proj_weight, mlp_gain, mlp_up, mlp_down
    )
    return return_part(exchange(leaving), slot)


def solution(mesh):
    both = P(("slab", "tile"))
    in_specs = (
        P(("slab", "tile"), None), P(None, ("slab", "tile")), P(None, ("slab", "tile")), both, both,
    ) + (P(),) * 9
    mapped = jax.shard_map(
        local, mesh=mesh, in_specs=in_specs, out_specs=P(("slab", "tile"), None), check_vma=False
    )

    def run(*args):
        with jax.sharding.use_abstract_mesh(mesh.abstract_mesh):
            return mapped(*args)

    return run
```

```python
import math

import jax
import jax.numpy as jnp
from jax import lax
from jax.experimental import pallas as pl
from jax.experimental.pallas import tpu as pltpu
from jax.sharding import PartitionSpec as P

EPS = 1e-05
F32 = jnp.float32
BF16 = jnp.bfloat16
I32 = jnp.int32

C = 256
HEADS = 8
HEAD_DIM = 32
PATCH = 1024
ROWS = 2048
RIM = 128
PEERS = 128
CAP = 24
SLOTS = PEERS * CAP
OFFSETS = 27
GROUP = 9
BLOCK = 128
WINDOW = 256
SUPER = 1024
TOGETHER = 4
OUT_CHUNK = 768
SEQ_CHUNK = 256
LEAVE_CHUNK = 512
RETURN_ROWS = 1024
QBLOCK = 512
SCORE_SCALE = math.log2(math.e) / math.sqrt(HEAD_DIM)
GELU_A = math.sqrt(2.0 / math.pi)
GELU_B = 0.044715 * GELU_A


def dot(a, b):
    return jnp.dot(a, b, preferred_element_type=F32)


def dot_nt(a, b):
    return lax.dot_general(a, b, (((1,), (1,)), ((), ())), preferred_element_type=F32)


def layer_norm(values, gain):
    centred = values - jnp.mean(values, axis=-1, keepdims=True)
    spread = jnp.mean(centred * centred, axis=-1, keepdims=True)
    return centred * lax.rsqrt(spread + EPS) * gain


def offset(place, base):
    return jnp.clip(place - base, -1, WINDOW).astype(F32).astype(BF16)


def small_iota(shape, axis):
    base = lax.broadcasted_iota(I32, shape, axis)
    return base.astype(F32).astype(BF16)


def hits(place, iota):
    return jnp.where(place == iota, jnp.ones((), BF16), jnp.zeros((), BF16))


def columns(place, count):
    base = jnp.arange(count // WINDOW, dtype=I32) * WINDOW
    return offset(place.reshape(-1, 1), base.reshape(1, -1))


def near(array):
    return pltpu.with_memory_space_constraint(array, pltpu.VMEM)


def whole(shape):
    return pl.BlockSpec(shape, lambda i, *_: (0,) * len(shape))


def conv_kernel(
    first_ref, count_ref, most_ref, own, lower, upper, index, valid, owners, weight_hbm, cpe, gain,
    outgoing, slot, ext, picked, weight, emb, sem,
):
    fetch = pltpu.make_async_copy(weight_hbm, weight, sem)
    fetch.start()
    ext[0:RIM, :] = lower[...]
    ext[RIM : RIM + ROWS, :] = own[...]
    ext[RIM + ROWS : 2 * RIM + ROWS, :] = upper[...]
    ext[2 * RIM + ROWS :, :] = jnp.zeros((WINDOW, C), BF16)
    lanes = small_iota((BLOCK, WINDOW), 1)

    def place(b):
        row = pl.multiple_of(b * BLOCK, BLOCK)
        cols = pl.ds(row, BLOCK)
        return row, jnp.transpose(jnp.where(valid[:, cols] > 0, index[:, cols], -1).astype(F32), (1, 0))

    def window(row, columns, g, entry, t):
        base = pl.multiple_of(first_ref[entry] + t * WINDOW, 16)
        rels = jnp.clip(columns - base.astype(F32), -1.0, float(WINDOW)).astype(BF16)
        chosen = [hits(rels[:, GROUP * g + k : GROUP * g + k + 1], lanes) for k in range(GROUP)]
        rows = dot(jnp.concatenate(chosen, axis=0), ext[pl.ds(base, WINDOW), :]).astype(BF16)
        return [
            ((pl.ds(row, BLOCK), slice((GROUP * g + k) * C, (GROUP * g + k + 1) * C)), rows[k * BLOCK : (k + 1) * BLOCK, :])
            for k in range(GROUP)
        ]

    def build(b):
        row, columns = place(b)
        for g in range(OFFSETS // GROUP):
            for dst, rows in window(row, columns, g, g * (ROWS // BLOCK) + b, 0):
                picked[dst] = rows

    def build_rest(b, carry):
        row, columns = place(b)
        for g in range(OFFSETS // GROUP):

            def more(t, carry):
                for dst, rows in window(row, columns, g, g * (ROWS // BLOCK) + b, t):
                    picked[dst] = picked[dst] + rows
                return carry

            lax.fori_loop(1, count_ref[g * (ROWS // BLOCK) + b], more, 0)
        return carry

    def some_blocks(i, carry):
        for j in range(TOGETHER):
            build(i * TOGETHER + j)
        return carry

    lax.fori_loop(0, ROWS // BLOCK // TOGETHER, some_blocks, 0)

    @pl.when(most_ref[0] > 1)
    def _():
        lax.fori_loop(0, ROWS // BLOCK, build_rest, 0)

    fetch.wait()

    width = 256
    peer = lax.broadcasted_iota(I32, (PEERS, width), 0)
    before = lax.broadcasted_iota(I32, (width, width), 0) < lax.broadcasted_iota(I32, (width, width), 1)
    before = jnp.where(before, 1.0, 0.0).astype(BF16)
    base = jnp.zeros((PEERS, 1), F32)
    for c in range(ROWS // width):
        cols = slice(c * width, (c + 1) * width)
        owner = owners[:, cols]
        mine = jnp.where(peer == owner, 1.0, 0.0)
        seen = dot(mine.astype(BF16), before) + base
        rank = jnp.sum(mine * seen, axis=0, keepdims=True)
        slot[:, cols] = owner * CAP + rank.astype(I32)
        base = base + jnp.sum(mine, axis=1, keepdims=True)

    for c in range(ROWS // SUPER):
        rows = slice(c * SUPER, (c + 1) * SUPER)
        linear = dot(dot(picked[rows, :], weight[...]).astype(BF16), cpe[...])
        emb[rows, :] = (own[rows, :].astype(F32) + layer_norm(linear, gain[...])).astype(BF16)

    places = small_iota((WINDOW, ROWS), 0)
    for c in range(SLOTS // OUT_CHUNK):
        at = (c % 2) * OUT_CHUNK
        for w in range(OUT_CHUNK // WINDOW):
            picked[at + w * WINDOW : at + (w + 1) * WINDOW, 0:ROWS] = hits(offset(slot[...], c * OUT_CHUNK + w * WINDOW), places)
        outgoing[c * OUT_CHUNK : (c + 1) * OUT_CHUNK, :] = dot(picked[at : at + OUT_CHUNK, 0:ROWS], emb[...]).astype(BF16)


def conv_part(features, lower, upper, neighbours, validity, owners, conv_weight, cpe_weight, cpe_gain):
    index = jnp.where(validity > 0, neighbours, -1)
    split = (OFFSETS // GROUP, GROUP, ROWS // BLOCK, BLOCK)
    low = jnp.min(jnp.where(validity > 0, neighbours, 2 * ROWS).reshape(split), axis=(1, 3))
    high = jnp.max(index.reshape(split), axis=(1, 3))
    low = jnp.minimum(low, ROWS + 2 * RIM - 1) & -16
    count = (high - low + WINDOW) >> 8
    args = (
        low.reshape(-1), count.reshape(-1), jnp.max(count).reshape(1), features, lower, upper, neighbours, validity, owners.reshape(1, ROWS),
        conv_weight.reshape(OFFSETS * C, C), cpe_weight, cpe_gain.reshape(1, C),
    )
    spaces = [pltpu.SMEM] * 3 + [pltpu.VMEM] * 6 + [pl.ANY] + [pltpu.VMEM] * 2
    return pl.pallas_call(
        conv_kernel,
        in_specs=[pl.BlockSpec(memory_space=m) for m in spaces],
        out_specs=[pl.BlockSpec(memory_space=pltpu.VMEM)] * 2,
        scratch_shapes=[
            pltpu.VMEM((ROWS + 2 * RIM + WINDOW, C), BF16),
            pltpu.VMEM((ROWS, OFFSETS * C), BF16),
            pltpu.VMEM((OFFSETS * C, C), BF16),
            pltpu.VMEM((ROWS, C), BF16),
            pltpu.SemaphoreType.DMA(()),
        ],
        out_shape=[jax.ShapeDtypeStruct((SLOTS, C), BF16), jax.ShapeDtypeStruct((1, ROWS), I32)],
        compiler_params=pltpu.CompilerParams(vmem_limit_bytes=52 << 20),
        name="conv_part",
    )(*args)


def attend_kernel(
    arrived, table_row, table_col, attn_gain, qkv, proj, mlp_gain, up, down,
    leaving, seq, processed, keys, queries, values, mixed, scores_a, scores_b, peak_a, peak_b,
):
    patch = pl.program_id(0)
    places = small_iota((WINDOW, SLOTS), 0)
    for c in range(PATCH // SEQ_CHUNK):
        rows = slice(c * SEQ_CHUNK, (c + 1) * SEQ_CHUNK)
        pick = [
            hits(offset(table_row[...], patch * PATCH + c * SEQ_CHUNK + w), places) for w in range(0, SEQ_CHUNK, WINDOW)
        ]
        seq[rows, :] = dot(jnp.concatenate(pick, axis=0), arrived[...])
    normed = layer_norm(seq[...], attn_gain[...]).astype(BF16)
    queries[...] = dot_nt(jnp.transpose(qkv[:, 0:C], (1, 0)), normed).astype(BF16)
    key_rows = dot(normed, qkv[:, C : 2 * C]).astype(BF16)
    value_cols = dot_nt(jnp.transpose(qkv[:, 2 * C :], (1, 0)), normed).astype(BF16)
    for h in range(HEADS):
        keys[h, :, :] = key_rows[:, HEAD_DIM * h : HEAD_DIM * (h + 1)]
        values[h, 0:HEAD_DIM, :] = value_cols[HEAD_DIM * h : HEAD_DIM * (h + 1), :]
        values[h, HEAD_DIM:, :] = jnp.ones((16, PATCH), BF16)
    per_head = PATCH // QBLOCK
    tasks = HEADS * per_head

    def where_is(t):
        head = lax.div(t, per_head)
        return (
            head,
            pl.multiple_of(head * HEAD_DIM, HEAD_DIM),
            pl.multiple_of(lax.rem(t, per_head) * QBLOCK, QBLOCK),
        )

    def score(t, scores, peak):
        head, row, col = where_is(lax.rem(t, tasks))
        found = dot(keys[head], queries[pl.ds(row, HEAD_DIM), pl.ds(col, QBLOCK)])
        scores[...] = found
        peak[...] = jnp.max(found, axis=0, keepdims=True)

    def mix(t, scores, peak):
        head, row, col = where_is(t)
        raised = jnp.exp2(((scores[...] - peak[...]) * SCORE_SCALE).astype(BF16))
        total = dot(values[head], raised)
        mixed[pl.ds(row, HEAD_DIM), pl.ds(col, QBLOCK)] = total[0:HEAD_DIM, :] / total[HEAD_DIM : HEAD_DIM + 1, :]

    score(0, scores_a, peak_a)

    def one(t, carry):
        @pl.when(lax.rem(t, 2) == 0)
        def _():
            score(t + 1, scores_b, peak_b)
            mix(t, scores_a, peak_a)

        @pl.when(lax.rem(t, 2) == 1)
        def _():
            score(t + 1, scores_a, peak_a)
            mix(t, scores_b, peak_b)

        return carry

    lax.fori_loop(0, tasks, one, 0)
    attended = jnp.transpose(mixed[...], (1, 0)).astype(BF16)
    after = (seq[...] + dot(attended, proj[...])).astype(BF16).astype(F32)
    normed_two = layer_norm(after, mlp_gain[...]).astype(BF16)
    wide = dot(normed_two, up[...])
    inner = wide * (GELU_A + GELU_B * (wide * wide))
    hidden = (wide + wide * jnp.tanh(inner)).astype(BF16)
    at = pl.multiple_of(patch * PATCH, PATCH)
    processed[pl.ds(at, PATCH), :] = (after + 0.5 * dot(hidden, down[...])).astype(BF16)

    @pl.when(patch == ROWS // PATCH - 1)
    def _():
        chunk = LEAVE_CHUNK
        lanes = small_iota((chunk, WINDOW), 1)
        for c in range(SLOTS // chunk):
            rows = slice(c * chunk, (c + 1) * chunk)
            pick = [hits(table_col[rows, w : w + 1], lanes) for w in range(ROWS // WINDOW)]
            leaving[rows, :] = dot(jnp.concatenate(pick, axis=1), processed[...]).astype(BF16)


def attend_part(arrived, slot_table, attn_gain, qkv_weight, proj_weight, mlp_gain, mlp_up, mlp_down):
    args = (
        arrived, slot_table.reshape(1, SLOTS), near(columns(slot_table, ROWS)), attn_gain.reshape(1, C),
        qkv_weight, proj_weight, mlp_gain.reshape(1, C), near(mlp_up), near(mlp_down),
    )
    return pl.pallas_call(
        attend_kernel,
        grid=(ROWS // PATCH,),
        in_specs=[pl.BlockSpec(memory_space=pltpu.VMEM) for a in args],
        out_specs=pl.BlockSpec(memory_space=pltpu.VMEM),
        out_shape=jax.ShapeDtypeStruct((SLOTS, C), BF16),
        scratch_shapes=[
            pltpu.VMEM((PATCH, C), F32),
            pltpu.VMEM((ROWS, C), BF16),
            pltpu.VMEM((HEADS, PATCH, HEAD_DIM), BF16),
            pltpu.VMEM((C, PATCH), BF16),
            pltpu.VMEM((HEADS, HEAD_DIM + 16, PATCH), BF16),
            pltpu.VMEM((C, PATCH), F32),
            pltpu.VMEM((PATCH, QBLOCK), F32),
            pltpu.VMEM((PATCH, QBLOCK), F32),
            pltpu.VMEM((1, QBLOCK), F32),
            pltpu.VMEM((1, QBLOCK), F32),
        ],
        compiler_params=pltpu.CompilerParams(vmem_limit_bytes=52 << 20),
        name="attend_part",
    )(*args)


def return_kernel(returned, slot_col, out):
    count = out.shape[0]
    lanes = small_iota((count, WINDOW), 1)
    rows = pl.ds(pl.multiple_of(pl.program_id(0) * count, count), count)
    pick = [hits(slot_col[rows, w : w + 1], lanes) for w in range(SLOTS // WINDOW)]
    out[...] = dot(jnp.concatenate(pick, axis=1), returned[...]).astype(BF16)


def return_part(returned, slot):
    rows = RETURN_ROWS
    return pl.pallas_call(
        return_kernel,
        grid=(ROWS // rows,),
        in_specs=[pl.BlockSpec(memory_space=pltpu.VMEM)] * 2,
        out_specs=pl.BlockSpec((rows, C), lambda i: (i, 0)),
        out_shape=jax.ShapeDtypeStruct((ROWS, C), BF16),
        compiler_params=pltpu.CompilerParams(vmem_limit_bytes=52 << 20),
        name="return_part",
    )(returned, near(columns(slot, SLOTS)))


def exchange(rows):
    rows = lax.all_to_all(
        rows.reshape(PEERS, CAP, C), ("slab", "tile"), split_axis=0, concat_axis=0, tiled=True
    ).reshape(SLOTS, C)
    return near(rows)


def local(
    features, neighbours, validity, owners, slot_table, conv_weight, cpe_weight, cpe_gain,
    attn_gain, qkv_weight, proj_weight, mlp_gain, mlp_up, mlp_down,
):
    slabs = lax.axis_size("slab")
    lower = lax.ppermute(features[ROWS - RIM :], "slab", [(i, i + 1) for i in range(slabs - 1)])
    upper = lax.ppermute(features[:RIM], "slab", [(i + 1, i) for i in range(slabs - 1)])
    outgoing, slot = conv_part(
        features, lower, upper, neighbours, validity, owners, conv_weight, cpe_weight, cpe_gain
    )
    leaving = attend_part(
        exchange(outgoing), slot_table, attn_gain, qkv_weight, proj_weight, mlp_gain, mlp_up, mlp_down
    )
    return return_part(exchange(leaving), slot)


def solution(mesh):
    both = P(("slab", "tile"))
    in_specs = (
        P(("slab", "tile"), None), P(None, ("slab", "tile")), P(None, ("slab", "tile")), both, both,
    ) + (P(),) * 9
    mapped = jax.shard_map(
        local, mesh=mesh, in_specs=in_specs, out_specs=P(("slab", "tile"), None), check_vma=False
    )

    def run(*args):
        with jax.sharding.use_abstract_mesh(mesh.abstract_mesh):
            return mapped(*args)

    return run
```
